32 devices in a mesh: fsdp: 8 (over y, x, core), rep: 4 (over z).
Axes of the slice: x: 2, y: 2, z: 4, core: 2. Of those that a mesh axis runs over, the one named last changes fastest.
Arguments:
- tokens: bfloat16 [32, 1024, 1152], P(('fsdp', 'rep')), may hold values from -6 to 6
- condition: bfloat16 [32, 4, 1152], P(('fsdp', 'rep')), may hold values from -6 to 6
- heights: int32 [32, 4], P(('fsdp', 'rep')), may hold values from 8 to 16, as said below
- widths: int32 [32, 4], P(('fsdp', 'rep')), may hold values from 8 to 16, as said below
- lengths: int32 [32, 4], P(('fsdp', 'rep')), may hold values from 64 to 256, as said below
- segments: int32 [32, 1024], P(('fsdp', 'rep')), may hold values from 0 to 4, as said below
- ada_weight: float32 [1152, 6912], P('fsdp'), may hold values from -0.1875 to 0.1875
- ada_bias: float32 [6912], P('fsdp'), may hold values from -3 to 3
- qkv_weight: float32 [1152, 3456], P('fsdp'), may hold values from -0.1875 to 0.1875
- out_weight: float32 [1152, 1152], P('fsdp'), may hold values from -0.75 to 0.75
- gate_up_weight: float32 [1152, 6144], P('fsdp'), may hold values from -0.1875 to 0.1875
- down_weight: float32 [3072, 1152], P('fsdp'), may hold values from -0.109375 to 0.109375
- query_gain: float32 [72], replicated, may hold values from 1 to 2
- key_gain: float32 [72], replicated, may hold values from 1 to 2
- cotangent: bfloat16 [32, 1024, 1152], P(('fsdp', 'rep')), may hold values from -6 to 6
Outputs:
- out: bfloat16 [32, 1024, 1152], P(('fsdp', 'rep'))
- grad_tokens: bfloat16 [32, 1024, 1152], P(('fsdp', 'rep'))
- grad_condition: bfloat16 [32, 4, 1152], P(('fsdp', 'rep'))
- grad_ada_weight: float32 [1152, 6912], P('fsdp')
- grad_ada_bias: float32 [6912], P('fsdp')
- grad_qkv_weight: float32 [1152, 3456], P('fsdp')
- grad_out_weight: float32 [1152, 1152], P('fsdp')
- grad_gate_up_weight: float32 [1152, 6144], P('fsdp')
- grad_down_weight: float32 [3072, 1152], P('fsdp')
- grad_query_gain: float32 [72], replicated
- grad_key_gain: float32 [72], replicated
The draws below stay inside these ranges and needn't reach their ends.
Inputs may be any that keep to these rules, and one draw needn't show every extreme that they name: `heights`: the first image of every sequence has 16 rows. `widths`: the first image of every sequence has 16 columns and the second half of 16. `lengths`: each length is that image's rows times its columns; the images of a sequence lie one after another from position 0 and leave padding at its end. `segments`: image i holds the positions given by lengths, in order; the positions after the last image are padding with number 4.
All inputs are finite; a program needn't handle non-finite values.
Results may differ from the reference program's by a relative error of at most 0.019.
The reference program's roundings to bfloat16 on the way count: a program that leaves them out, or rounds other values in their place, can miss the bound.
Values may be sent and summed in bfloat16 or wider, within the bound.
A program may use at most 320 MiB of HBM per device.

```python
import math
import jax
import jax.numpy as jnp
from jax import lax

D = 1152
HEADS = 16
HEAD_DIM = 72
FF = 3072
ITEMS = 4
GRID = 16
SEQ_LEN = 1024
SEQS = 32


def image_layout(key):
    salted = jax.random.fold_in(key, 4242)
    key_rows, key_cols = jax.random.split(salted)
    heights = jax.random.randint(key_rows, (SEQS, ITEMS), GRID // 2, GRID + 1, dtype=jnp.int32)
    widths = jax.random.randint(key_cols, (SEQS, ITEMS), GRID // 2, GRID + 1, dtype=jnp.int32)
    heights = heights.at[:, 0].set(GRID)
    widths = widths.at[:, 0].set(GRID).at[:, 1].set(GRID // 2)
    lengths = heights * widths
    ends = jnp.cumsum(lengths, axis=1).astype(jnp.int32)
    places = jnp.arange(SEQ_LEN, dtype=jnp.int32)
    segments = jnp.sum((ends[:, None, :] <= places[None, :, None]).astype(jnp.int32), axis=2).astype(jnp.int32)
    return (heights, widths, lengths, segments)


def draw_heights(key, part):
    return image_layout(key)[0]


def draw_widths(key, part):
    return image_layout(key)[1]


def draw_lengths(key, part):
    return image_layout(key)[2]


def draw_segments(key, part):
    return image_layout(key)[3]


def block_levels(stream_key, shape, shards, smallest, top_value):
    level, own = 1.0, jax.random.fold_in(stream_key, 6)
    for axis_at, shards_of in shards:
        steps = jnp.exp(jax.random.uniform(jax.random.fold_in(own, axis_at), (shards_of,), jnp.float32, smallest / len(shards), top_value / len(shards)))
        level = level * jnp.repeat(steps, shape[axis_at] // shards_of).reshape([-1 if axis == axis_at else 1 for axis in range(len(shape))])
    return level


def normal_values(key, extent, deviation, limit, shards=(), kind=jnp.bfloat16):
    level = block_levels(key, extent, shards, -0.22, 0.18) if shards else 1.0
    values = jax.random.normal(key, extent, jnp.float32) * deviation * level
    return jnp.minimum(jnp.maximum(values, -limit), limit).astype(kind)


def setup_inputs(seed: int = 0) -> dict:
    key_list = jax.random.split(jax.random.key(seed), 16)
    return {
        "tokens": normal_values(key_list[0], (SEQS, SEQ_LEN, D), 1.0, 6.0, ((0, 32),)),
        "condition": normal_values(key_list[1], (SEQS, ITEMS, D), 1.0, 6.0, ((0, 32),)),
        "heights": draw_heights(jax.random.fold_in(key_list[15], 71), 0),
        "widths": draw_widths(jax.random.fold_in(key_list[15], 71), 0),
        "lengths": draw_lengths(jax.random.fold_in(key_list[15], 71), 0),
        "segments": draw_segments(jax.random.fold_in(key_list[15], 71), 0),
        "ada_weight": normal_values(key_list[6], (D, 6 * D), D ** -0.5, 0.1875, ((0, 8),), jnp.float32),
        "ada_bias": normal_values(key_list[7], (6 * D,), 0.5, 3.0, ((0, 8),), jnp.float32),
        "qkv_weight": normal_values(key_list[8], (D, 3 * D), D ** -0.5, 0.1875, ((0, 8),), jnp.float32),
        "out_weight": normal_values(key_list[9], (D, D), (D // 16) ** -0.5, 0.75, ((0, 8),), jnp.float32),
        "gate_up_weight": normal_values(key_list[10], (D, 2 * FF), D ** -0.5, 0.1875, ((0, 8),), jnp.float32),
        "down_weight": normal_values(key_list[11], (FF, D), FF ** -0.5, 0.109375, ((0, 8),), jnp.float32),
        "query_gain": jnp.clip(jnp.exp(jax.random.uniform(key_list[12], (HEAD_DIM,), jnp.float32, math.log(1.0), math.log(2.0))), 1.0, 2.0),
        "key_gain": jnp.clip(jnp.exp(jax.random.uniform(key_list[13], (HEAD_DIM,), jnp.float32, math.log(1.0), math.log(2.0))), 1.0, 2.0),
        "cotangent": normal_values(key_list[14], (SEQS, SEQ_LEN, D), 1.0, 6.0, ((0, 32),)),
    }


@jax.custom_vjp
def low(v):
    return lax.optimization_barrier(v.astype(jnp.bfloat16)).astype(jnp.float32)

@jax.custom_vjp
def low_back(v):
    return v

def low_keep(v):
    return (low(v), None)

def low_pass(kept, grad):
    return (grad,)

def back_keep(v):
    return (v, None)

def back_low(kept, grad):
    return (low(grad),)
low.defvjp(low_keep, low_pass)
low_back.defvjp(back_keep, back_low)
highest = lax.Precision.HIGHEST
epsilon = 1e-06

def grid_tables(heights_one, widths_one, lengths_one, segment_one):
    ends = jnp.cumsum(lengths_one).astype(jnp.int32)
    starts = ends - lengths_one
    places = jnp.arange(SEQ_LEN, dtype=jnp.int32)
    member = segment_one[:, None] == jnp.arange(ITEMS, dtype=jnp.int32)[None, :]
    start_tok = lax.optimization_barrier(jnp.sum(jnp.where(member, starts[None, :], 0), axis=1)).astype(jnp.int32)
    width_tok = lax.optimization_barrier(jnp.sum(jnp.where(member, widths_one[None, :], 0), axis=1)).astype(jnp.int32)
    height_tok = lax.optimization_barrier(jnp.sum(jnp.where(member, heights_one[None, :], 0), axis=1)).astype(jnp.int32)
    inside = width_tok > 0
    offset = places - start_tok
    safe_width = jnp.maximum(width_tok, 1)
    safe_height = jnp.maximum(height_tok, 1)
    row_index = jnp.where(inside, offset // safe_width, 0)
    col_index = jnp.where(inside, offset % safe_width, 0)
    height_f = safe_height.astype(jnp.float32)
    width_f = safe_width.astype(jnp.float32)
    row_place = jnp.where(inside, (row_index.astype(jnp.float32) - 0.5 * (height_f - 1.0)) * (GRID / height_f), 0.0)
    col_place = jnp.where(inside, (col_index.astype(jnp.float32) - 0.5 * (width_f - 1.0)) * (GRID / width_f), 0.0)
    quarter = HEAD_DIM // 4
    freqs = jnp.exp(jnp.arange(quarter, dtype=jnp.float32) * (-math.log(10000.0) / quarter))
    row_angle = row_place[:, None] * freqs[None, :]
    col_angle = col_place[:, None] * freqs[None, :]
    return (member.astype(jnp.float32), jnp.cos(row_angle), jnp.sin(row_angle), jnp.cos(col_angle), jnp.sin(col_angle))

def rotate(values, tables, sign):
    quarter = values.shape[-1] // 4
    first = values[..., :quarter]
    second = values[..., quarter:2 * quarter]
    third = values[..., 2 * quarter:3 * quarter]
    fourth = values[..., 3 * quarter:]
    cos_row, sin_row, cos_col, sin_col = [t[..., None, :] for t in tables]
    return jnp.concatenate([first * cos_row - sign * second * sin_row, second * cos_row + sign * first * sin_row, third * cos_col - sign * fourth * sin_col, fourth * cos_col + sign * third * sin_col], axis=-1)

def head_norm(values):
    return values * lax.rsqrt(lax.optimization_barrier(jnp.mean(values * values, axis=-1, keepdims=True)) + epsilon)

def attention(query, keys, values, segment_group):
    group = query.shape[0]
    block_rows = min(512, SEQ_LEN)
    blocks = SEQ_LEN // block_rows
    score_scale = HEAD_DIM ** (-0.5)
    query_blocks = query.reshape(group, blocks, block_rows, HEADS, HEAD_DIM).transpose(1, 0, 2, 3, 4)
    segment_blocks = segment_group.reshape(group, blocks, block_rows).transpose(1, 0, 2)

    def one_block(pair):
        query_b, segment_b = pair
        scores = low_back(jnp.einsum('gqhd,gkhd->ghqk', query_b, keys, precision=highest) * score_scale)
        allowed = segment_b[:, None, :, None] == segment_group[:, None, None, :]
        scores = jnp.where(allowed, scores, -1000000000.0)
        chance = jax.nn.softmax(scores, axis=-1)
        return jnp.einsum('ghqk,gkhd->gqhd', low(chance), values, precision=highest)
    result = lax.map(jax.checkpoint(one_block), (query_blocks, segment_blocks))
    return result.transpose(1, 0, 2, 3, 4).reshape(group, SEQ_LEN, D)

def forward(weights, tokens, condition, member, tables, segment_group):
    ada_weight, ada_bias, qkv_weight, out_weight, gate_up_weight, down_weight, query_gain, key_gain = weights
    group = tokens.shape[0]
    cond_act = low(jax.nn.silu(condition))
    modulation = low_back(jnp.einsum('gid,de->gie', cond_act, low(ada_weight), precision=highest) + low(ada_bias))
    per_token = jnp.einsum('gti,gie->gte', member, modulation, precision=highest)
    shift_a, scale_a, gate_a, shift_b, scale_b, gate_b = jnp.split(per_token, 6, axis=-1)
    normed_a = tokens * lax.rsqrt(lax.optimization_barrier(jnp.mean(tokens * tokens, axis=-1, keepdims=True)) + epsilon)
    hidden_a = low(normed_a * (1.0 + scale_a) + shift_a)
    projected = low_back(jnp.einsum('gtd,de->gte', hidden_a, low(qkv_weight), precision=highest))
    query_raw, key_raw, value_raw = jnp.split(projected, 3, axis=-1)
    head_shape = (group, SEQ_LEN, HEADS, HEAD_DIM)
    query = low(rotate(head_norm(query_raw.reshape(head_shape)) * query_gain, tables, 1.0))
    keys = low(rotate(head_norm(key_raw.reshape(head_shape)) * key_gain, tables, 1.0))
    values = low(value_raw.reshape(head_shape))
    attended = low(low_back(attention(query, keys, values, segment_group)))
    branch_a = low_back(jnp.einsum('gtd,de->gte', attended, low(out_weight), precision=highest))
    stream_b = tokens + gate_a * branch_a
    normed_b = stream_b * lax.rsqrt(lax.optimization_barrier(jnp.mean(stream_b * stream_b, axis=-1, keepdims=True)) + epsilon)
    hidden_b = low(normed_b * (1.0 + scale_b) + shift_b)
    gate_up = low_back(jnp.einsum('gtd,de->gte', hidden_b, low(gate_up_weight), precision=highest))
    gate_val, up_val = jnp.split(gate_up, 2, axis=-1)
    inner = low(jax.nn.silu(gate_val) * up_val)
    branch_b = low_back(jnp.einsum('gtf,fd->gtd', inner, low(down_weight), precision=highest))
    return stream_b + gate_b * branch_b

def reference(tokens, condition, heights, widths, lengths, segments, ada_weight, ada_bias, qkv_weight, out_weight, gate_up_weight, down_weight, query_gain, key_gain, cotangent):
    weights = tuple((w.astype(jnp.float32) for w in (ada_weight, ada_bias, qkv_weight, out_weight, gate_up_weight, down_weight, query_gain, key_gain)))
    member, cos_row, sin_row, cos_col, sin_col = jax.vmap(grid_tables)(heights, widths, lengths, segments)
    group = 4
    rounds = SEQS // group

    def regroup(array):
        return array.reshape((rounds, group) + array.shape[1:])

    def step(totals, batch):
        tokens_group, cond_group, member_group, table_group, segment_group, cot_group = batch

        def run(weight_set, tokens_in, cond_in):
            return forward(weight_set, tokens_in, cond_in, member_group, table_group, segment_group)
        result, pullback = jax.vjp(run, weights, tokens_group.astype(jnp.float32), cond_group.astype(jnp.float32))
        grad_weights, grad_tok, grad_cond = pullback(cot_group.astype(jnp.float32))
        totals = tuple((a + b for a, b in zip(totals, grad_weights)))
        return (totals, (result.astype(jnp.bfloat16), grad_tok.astype(jnp.bfloat16), grad_cond.astype(jnp.bfloat16)))
    zeros = tuple((jnp.zeros_like(w) for w in weights))
    batches = (regroup(tokens), regroup(condition), regroup(member), (regroup(cos_row), regroup(sin_row), regroup(cos_col), regroup(sin_col)), regroup(segments), regroup(cotangent))
    totals, (result, grad_tok, grad_cond) = lax.scan(step, zeros, batches)
    return (result.reshape(tokens.shape), grad_tok.reshape(tokens.shape), grad_cond.reshape(condition.shape), totals[0], totals[1], totals[2], totals[3], totals[4], totals[5], totals[6], totals[7])
```

```python
import functools
import math

import jax
import jax.numpy as jnp
from jax import lax
from jax.experimental import pallas as pl
from jax.experimental.pallas import tpu as pltpu
from jax.sharding import PartitionSpec as P

D = 1152
HEADS = 16
HEAD_DIM = 72
SEQ_LEN = 1024
FF = 3072
ITEMS = 4
GRID = 16
epsilon = 1e-06
PAD = 24
FIRST = 256
BLK = 256
SCORE_EXP = HEAD_DIM ** (-0.5) * math.log2(math.e)
f32 = jnp.float32
bf16 = jnp.bfloat16


def dot_nn(a, b):
    return lax.dot_general(a, b, (((1,), (0,)), ((), ())), preferred_element_type=f32)


def dot_nt(a, b):
    return lax.dot_general(a, b, (((1,), (1,)), ((), ())), preferred_element_type=f32)


def block_at(index):
    return pl.ds(pl.multiple_of(index * BLK, BLK), BLK)


def turn(value, roll_ref, cos_t, up_t, down_t, sign):
    roll_ref[PAD : PAD + HEAD_DIM, :] = value
    above = roll_ref[PAD + 18 : PAD + 18 + HEAD_DIM, :]
    below = roll_ref[PAD - 18 : PAD - 18 + HEAD_DIM, :]
    return value * cos_t + sign * (above * up_t + below * down_t)


def normed(raw):
    factor = lax.rsqrt(jnp.sum(raw * raw, axis=0, keepdims=True) * (1.0 / HEAD_DIM) + epsilon)
    return raw * factor, factor


def fill_mask(seg_col_ref, seg_row_ref, mask_ref):
    for start in range(0, SEQ_LEN - FIRST, BLK):
        rows = seg_col_ref[FIRST + start : FIRST + start + BLK, :]
        cols = seg_row_ref[:, FIRST:]
        mask_ref[start : start + BLK, :] = jnp.where(rows == cols, 1.0, 0.0).astype(mask_ref.dtype)


def forward_kernel(q_ref, k_ref, v_ref, gq_ref, gk_ref, cos_ref, up_ref, down_ref, segc_ref, segr_ref,
                   o_ref, inv_ref, mask_ref, roll_ref, qt_ref, kk_ref, vt_ref):
    @pl.when(pl.program_id(0) == 0)
    def _():
        fill_mask(segc_ref, segr_ref, mask_ref)
        roll_ref[...] = jnp.zeros_like(roll_ref)

    for half in range(2):
        def prepare(index, carry):
            at = block_at(index)
            tables = (cos_ref[:, at], up_ref[:, at], down_ref[:, at])
            q_n, _ = normed(q_ref[half, :, at])
            qt_ref[half, :, at] = turn(q_n * gq_ref[...], roll_ref, *tables, 1.0).astype(bf16)
            k_n, _ = normed(k_ref[half, :, at])
            kk = turn(k_n * gk_ref[...], roll_ref, *tables, 1.0)
            kk_ref[half, at, :] = kk.T.astype(bf16)
            vt_ref[half, :, at] = v_ref[half, :, at].astype(bf16)
            return carry

        lax.fori_loop(0, SEQ_LEN // BLK, prepare, 0)

    def attend(at, lo, hi, mask):
        for half in range(2):
            scores = dot_nn(kk_ref[half, lo:hi, :], qt_ref[half, :, at])
            raised = jnp.exp2(scores * SCORE_EXP)
            if mask is not None:
                raised = raised * mask
            inverse = 1.0 / jnp.sum(raised, axis=0, keepdims=True)
            chance = (raised * inverse).astype(bf16)
            result = dot_nn(vt_ref[half, :, lo:hi], chance)
            o_ref[half * HEAD_DIM : (half + 1) * HEAD_DIM, at] = result.astype(bf16)
            inv_ref[half, :, at] = inverse

    attend(pl.ds(0, BLK), 0, FIRST, None)

    def later(index, carry):
        mask = mask_ref[:, block_at(index - 1)].astype(f32)
        attend(block_at(index), FIRST, SEQ_LEN, mask)
        return carry

    lax.fori_loop(1, SEQ_LEN // BLK, later, 0)


def backward_kernel(q_ref, k_ref, v_ref, g_ref, inv_ref, gq_ref, gk_ref, cos_ref, up_ref, down_ref, segc_ref,
                    segr_ref, d_ref, gain_ref, mask_ref, roll_ref, qt_ref, kt_ref, kk_ref, vv_ref,
                    dq_ref, dk_ref, dv_ref):
    @pl.when(pl.program_id(0) == 0)
    def _():
        fill_mask(segc_ref, segr_ref, mask_ref)
        roll_ref[...] = jnp.zeros_like(roll_ref)
        gain_ref[...] = jnp.zeros_like(gain_ref)

    for half in range(2):
        def prepare(index, carry):
            at = block_at(index)
            tables = (cos_ref[:, at], up_ref[:, at], down_ref[:, at])
            q_n, _ = normed(q_ref[half, :, at])
            qt_ref[half, :, at] = turn(q_n * gq_ref[...], roll_ref, *tables, 1.0).astype(bf16)
            k_n, _ = normed(k_ref[half, :, at])
            kk = turn(k_n * gk_ref[...], roll_ref, *tables, 1.0)
            kt_ref[half, :, at] = kk.astype(bf16)
            kk_ref[half, at, :] = kk.T.astype(bf16)
            vv_ref[half, at, :] = v_ref[half, :, at].T.astype(bf16)
            return carry

        lax.fori_loop(0, SEQ_LEN // BLK, prepare, 0)

    def attend(at, lo, hi, mask, first):
        for half in range(2):
            rows = slice(half * HEAD_DIM, (half + 1) * HEAD_DIM)
            q_b = qt_ref[half, :, at]
            g_b = g_ref[rows, at]
            scores = dot_nn(kk_ref[half, lo:hi, :], q_b)
            chance = jnp.exp2(scores * SCORE_EXP) * inv_ref[half, :, at]
            if mask is not None:
                chance = chance * mask
            grad_chance = dot_nn(vv_ref[half, lo:hi, :], g_b)
            delta = jnp.sum(chance * grad_chance, axis=0, keepdims=True)
            grad_scores = (chance * (grad_chance - delta)).astype(bf16)
            grad_v = dot_nt(g_b, chance.astype(bf16))
            grad_k = dot_nt(q_b, grad_scores)
            dq_ref[half, :, at] = dot_nn(kt_ref[half, :, lo:hi], grad_scores)
            if first:
                dv_ref[half, :, lo:hi] = grad_v
                dk_ref[half, :, lo:hi] = grad_k
            else:
                dv_ref[half, :, lo:hi] += grad_v
                dk_ref[half, :, lo:hi] += grad_k

    attend(pl.ds(0, BLK), 0, FIRST, None, True)
    dk_ref[:, :, FIRST:] = jnp.zeros((2, HEAD_DIM, SEQ_LEN - FIRST), f32)
    dv_ref[:, :, FIRST:] = jnp.zeros((2, HEAD_DIM, SEQ_LEN - FIRST), f32)

    def later(index, carry):
        mask = mask_ref[:, block_at(index - 1)].astype(f32)
        attend(block_at(index), FIRST, SEQ_LEN, mask, False)
        return carry

    lax.fori_loop(1, SEQ_LEN // BLK, later, 0)

    for half in range(2):
        rows = slice(half * HEAD_DIM, (half + 1) * HEAD_DIM)

        def finish(index, carry):
            at = block_at(index)
            tables = (cos_ref[:, at], up_ref[:, at], down_ref[:, at])
            for which, (raw_ref, grad_ref, weight_ref) in enumerate(((q_ref, dq_ref, gq_ref), (k_ref, dk_ref, gk_ref))):
                unit, factor = normed(raw_ref[half, :, at])
                grad = turn(grad_ref[half, :, at] * (HEAD_DIM ** -0.5), roll_ref, *tables, -1.0)
                part = grad * unit
                gain_ref[which] += part[:, :128] + part[:, 128:]
                grad = grad * weight_ref[...]
                mean = jnp.sum(grad * unit, axis=0, keepdims=True) * (1.0 / HEAD_DIM)
                d_ref[which, rows, at] = (factor * (grad - unit * mean)).astype(bf16)
            d_ref[2, rows, at] = dv_ref[half, :, at].astype(bf16)
            return carry

        lax.fori_loop(0, SEQ_LEN // BLK, finish, 0)


def whole(shape):
    return pl.BlockSpec(shape, lambda h: (0,) * len(shape))


def head_specs():
    return [pl.BlockSpec((2, HEAD_DIM, SEQ_LEN), lambda h, base=base: (base + h, 0, 0)) for base in (0, 8, 16)]


def table_specs():
    return [
        whole((HEAD_DIM, 1)), whole((HEAD_DIM, 1)),
        whole((HEAD_DIM, SEQ_LEN)), whole((HEAD_DIM, SEQ_LEN)), whole((HEAD_DIM, SEQ_LEN)),
        whole((SEQ_LEN, 1)), whole((1, SEQ_LEN)),
    ]


def work_scratch():
    return [
        pltpu.VMEM((SEQ_LEN - FIRST, SEQ_LEN - FIRST), bf16),
        pltpu.VMEM((HEAD_DIM + 2 * PAD, BLK), f32),
    ]


PAIR = (2, HEAD_DIM, SEQ_LEN)
TOKEN_PAIR = (2, SEQ_LEN, HEAD_DIM)


def attention_forward(raw, tables):
    return pl.pallas_call(
        forward_kernel,
        grid=(HEADS // 2,),
        in_specs=head_specs() + table_specs(),
        out_specs=[
            pl.BlockSpec((2 * HEAD_DIM, SEQ_LEN), lambda h: (h, 0)),
            pl.BlockSpec((2, 1, SEQ_LEN), lambda h: (h, 0, 0)),
        ],
        out_shape=[
            jax.ShapeDtypeStruct((D, SEQ_LEN), bf16),
            jax.ShapeDtypeStruct((HEADS, 1, SEQ_LEN), f32),
        ],
        scratch_shapes=work_scratch() + [
            pltpu.VMEM(PAIR, bf16), pltpu.VMEM(TOKEN_PAIR, bf16), pltpu.VMEM(PAIR, bf16),
        ],
        cost_estimate=pl.CostEstimate(flops=14_000_000_000, bytes_accessed=20_000_000, transcendentals=10_500_000),
        name="attend",
    )(raw, raw, raw, *tables)


def attention_backward(raw, grad_t, inverse, tables):
    return pl.pallas_call(
        backward_kernel,
        grid=(HEADS // 2,),
        in_specs=head_specs() + [
            pl.BlockSpec((2 * HEAD_DIM, SEQ_LEN), lambda h: (h, 0)),
            pl.BlockSpec((2, 1, SEQ_LEN), lambda h: (h, 0, 0)),
        ] + table_specs(),
        out_specs=[
            pl.BlockSpec((3, 2 * HEAD_DIM, SEQ_LEN), lambda h: (0, h, 0)),
            whole((2, HEAD_DIM, 128)),
        ],
        out_shape=[
            jax.ShapeDtypeStruct((3, D, SEQ_LEN), bf16),
            jax.ShapeDtypeStruct((2, HEAD_DIM, 128), f32),
        ],
        scratch_shapes=work_scratch() + [
            pltpu.VMEM(PAIR, bf16), pltpu.VMEM(PAIR, bf16), pltpu.VMEM(TOKEN_PAIR, bf16), pltpu.VMEM(TOKEN_PAIR, bf16),
            pltpu.VMEM(PAIR, f32), pltpu.VMEM(PAIR, f32), pltpu.VMEM(PAIR, f32),
        ],
        cost_estimate=pl.CostEstimate(flops=35_000_000_000, bytes_accessed=25_000_000, transcendentals=10_500_000),
        name="attend_back",
    )(raw, raw, raw, grad_t, inverse, *tables)


def product(left, right):
    return jnp.dot(left, right, preferred_element_type=f32)


def contract(left, right, left_dim, right_dim):
    return lax.dot_general(left, right, (((left_dim,), (right_dim,)), ((), ())), preferred_element_type=f32)


def angle_tables(heights, widths, lengths, segments):
    ends = jnp.cumsum(lengths)
    starts = ends - lengths
    places = jnp.arange(SEQ_LEN, dtype=jnp.int32)
    member = segments[:, None] == jnp.arange(ITEMS, dtype=jnp.int32)[None, :]
    start_tok = jnp.sum(jnp.where(member, starts[None, :], 0), axis=1)
    width_tok = jnp.sum(jnp.where(member, widths[None, :], 0), axis=1)
    height_tok = jnp.sum(jnp.where(member, heights[None, :], 0), axis=1)
    inside = width_tok > 0
    offset = places - start_tok
    safe_width = jnp.maximum(width_tok, 1)
    safe_height = jnp.maximum(height_tok, 1)
    row_index = jnp.where(inside, offset // safe_width, 0)
    col_index = jnp.where(inside, offset % safe_width, 0)
    height_f = safe_height.astype(f32)
    width_f = safe_width.astype(f32)
    row_place = jnp.where(inside, (row_index.astype(f32) - 0.5 * (height_f - 1.0)) * (GRID / height_f), 0.0)
    col_place = jnp.where(inside, (col_index.astype(f32) - 0.5 * (width_f - 1.0)) * (GRID / width_f), 0.0)
    quarter = HEAD_DIM // 4
    lane = jnp.arange(HEAD_DIM, dtype=jnp.int32)
    freqs = jnp.exp((lane % quarter).astype(f32) * (-math.log(10000.0) / quarter))
    place = jnp.where((lane < 2 * quarter)[:, None], row_place[None, :], col_place[None, :])
    angle = place * freqs[:, None]
    cos_t = jnp.cos(angle)
    sin_t = jnp.sin(angle)
    leading = (lane // quarter % 2 == 0)[:, None]
    return cos_t, jnp.where(leading, -sin_t, 0.0), jnp.where(leading, 0.0, sin_t)


def rms_scale(values):
    return lax.rsqrt(jnp.mean(values * values, axis=-1, keepdims=True) + epsilon)


def rms_back(grad_normed, normed_values, factor):
    return factor * (grad_normed - normed_values * jnp.mean(grad_normed * normed_values, axis=-1, keepdims=True))


def flip(array, axis, size, bit):
    return lax.ppermute(array, axis, [(i, i ^ bit) for i in range(size)])


def bits_of(size):
    return [1 << b for b in range(size.bit_length() - 1)]


def gather_steps(array, axis, size, dim):
    place = lax.axis_index(axis)
    for bit in bits_of(size):
        other = flip(array, axis, size, bit)
        low = (place & bit) == 0
        array = jnp.concatenate([jnp.where(low, array, other), jnp.where(low, other, array)], axis=dim)
    return array


def scatter_steps(array, axis, size):
    place = lax.axis_index(axis)
    for bit in bits_of(size):
        low = (place & bit) == 0
        pairs = array.reshape((array.shape[0] // 2, 2) + array.shape[1:])
        even, odd = pairs[:, 0], pairs[:, 1]
        received = flip(jnp.where(low, odd, even), axis, size, bit)
        array = jnp.where(low, even, odd) + received
    return array[0]


def butterfly_sum(array, axis, size):
    for bit in bits_of(size):
        array = array + flip(array, axis, size, bit)
    return array


def replica_sum(array, size, dim):
    place = lax.axis_index("rep")
    for bit in bits_of(size):
        low = (place & bit) == 0
        first, second = jnp.split(array, 2, axis=dim)
        received = flip(jnp.where(low, second, first), "rep", size, bit)
        array = (jnp.where(low, first, second).astype(f32) + received.astype(f32)).astype(bf16)
    for bit in reversed(bits_of(size)):
        low = (place & bit) == 0
        other = flip(array, "rep", size, bit)
        array = jnp.concatenate([jnp.where(low, array, other), jnp.where(low, other, array)], axis=dim)
    return array.astype(f32)


def per_device(
    fsdp,
    rep,
    tokens,
    condition,
    heights,
    widths,
    lengths,
    segments,
    ada_weight,
    ada_bias,
    qkv_weight,
    out_weight,
    gate_up_weight,
    down_weight,
    query_gain,
    key_gain,
    cotangent,
):
    place = lax.axis_index("fsdp")
    segment = segments[0]

    def gathered(weight):
        return lax.all_gather(weight.astype(bf16), "fsdp", axis=0, tiled=True)

    def scattered(grad):
        return lax.psum_scatter(grad.astype(bf16), "fsdp", scatter_dimension=0, tiled=True)

    qkv_full = gathered(qkv_weight)
    out_full = gathered(out_weight)
    gate_up_full = gathered(gate_up_weight)
    down_full = gathered(down_weight)

    shard = ada_weight.shape[0]
    cond_values = condition[0].astype(f32)
    cond_act = jax.nn.silu(cond_values).astype(bf16)
    cond_parts = cond_act.reshape(ITEMS, fsdp, shard).transpose(1, 0, 2)
    cond_cols = lax.all_to_all(cond_parts, "fsdp", 0, 0, tiled=True)
    ada_low = ada_weight.astype(bf16)
    partial = product(cond_cols.reshape(fsdp * ITEMS, shard), ada_low)
    bias_part = ada_bias.shape[0]
    bias_row = lax.dynamic_update_slice(
        jnp.zeros((6 * D,), f32), ada_bias.astype(bf16).astype(f32), (place * bias_part,)
    )
    modulation = scatter_steps((partial + bias_row[None, :]).reshape(fsdp, ITEMS, 6 * D), "fsdp", fsdp)

    segment_col = segment[:, None]

    def spread(which):
        rows = modulation[:, which * D : (which + 1) * D]
        result = jnp.zeros((SEQ_LEN, D), f32)
        for item in range(ITEMS):
            result = jnp.where(segment_col == item, rows[item][None, :], result)
        return result

    shift_a, scale_a, gate_a, shift_b, scale_b, gate_b = [spread(which) for which in range(6)]
    stream = tokens[0].astype(f32)
    factor_a = rms_scale(stream)
    normed_a = stream * factor_a
    hidden_a = (normed_a * (1.0 + scale_a) + shift_a).astype(bf16)
    raw = contract(qkv_full, hidden_a, 0, 1).reshape(3 * HEADS, HEAD_DIM, SEQ_LEN)
    tables = (
        query_gain[:, None],
        key_gain[:, None],
        *angle_tables(heights[0], widths[0], lengths[0], segment),
        segment_col,
        segment[None, :],
    )
    attended_t, inverse = attention_forward(raw, tables)
    branch_a = contract(attended_t, out_full, 0, 0)
    stream_b = stream + gate_a * branch_a
    factor_b = rms_scale(stream_b)
    normed_b = stream_b * factor_b
    hidden_b = (normed_b * (1.0 + scale_b) + shift_b).astype(bf16)
    gate_up = product(hidden_b, gate_up_full)
    gate_val = gate_up[:, :FF]
    up_val = gate_up[:, FF:]
    sigmoid_g = jax.nn.sigmoid(gate_val)
    inner = (gate_val * sigmoid_g * up_val).astype(bf16)
    branch_b = product(inner, down_full)
    result_tokens = (stream_b + gate_b * branch_b).astype(bf16)[None]

    upstream = cotangent[0].astype(f32)
    grad_gate_b = upstream * branch_b
    grad_branch_b = (upstream * gate_b).astype(bf16)
    grad_inner = contract(grad_branch_b, down_full, 1, 1)
    down_sum = scattered(contract(inner, grad_branch_b, 0, 0))
    grad_gate_val = grad_inner * up_val * sigmoid_g * (1.0 + gate_val * (1.0 - sigmoid_g))
    grad_up_val = grad_inner * gate_val * sigmoid_g
    grad_act = jnp.concatenate([grad_gate_val, grad_up_val], axis=1).astype(bf16)
    gate_up_sum = scattered(contract(hidden_b, grad_act, 0, 0))
    grad_hidden_b = contract(grad_act, gate_up_full, 1, 1)
    grad_scale_b = grad_hidden_b * normed_b
    grad_stream_b = upstream + rms_back(grad_hidden_b * (1.0 + scale_b), normed_b, factor_b)
    grad_gate_a = grad_stream_b * branch_a
    grad_branch_a = (grad_stream_b * gate_a).astype(bf16)
    out_sum = scattered(product(attended_t, grad_branch_a))
    grad_attended_t = contract(out_full, grad_branch_a, 1, 1).astype(bf16)
    grad_raw, gain_parts = attention_backward(raw, grad_attended_t, inverse, tables)
    grad_raw = grad_raw.reshape(3 * D, SEQ_LEN)
    qkv_sum = scattered(contract(hidden_a, grad_raw, 0, 1))
    grad_hidden_a = contract(grad_raw, qkv_full, 0, 1)
    stream_grad = grad_stream_b + rms_back(grad_hidden_a * (1.0 + scale_a), normed_a, factor_a)

    member = (segment[None, :] == jnp.arange(ITEMS, dtype=jnp.int32)[:, None]).astype(f32)

    def collect(piece):
        return jnp.dot(member, piece, precision=lax.Precision.HIGHEST).astype(bf16)

    def all_images(pieces):
        block = jnp.concatenate([collect(piece) for piece in pieces], axis=1)[None, None]
        return gather_steps(gather_steps(block, "rep", rep, 0), "fsdp", fsdp, 1)

    late_mod = all_images((grad_gate_a, grad_hidden_b, grad_scale_b, grad_gate_b))
    early_mod = all_images((grad_hidden_a, grad_hidden_a * normed_a))
    grad_mod = jnp.concatenate([early_mod, late_mod], axis=3)
    cond_all = gather_steps(cond_cols[None], "rep", rep, 0)
    images = rep * fsdp * ITEMS
    flat_mod = grad_mod.reshape(images, 6 * D)
    grad_ada = contract(cond_all.reshape(images, shard), flat_mod, 0, 0)
    bias_sum = jnp.sum(flat_mod.astype(f32), axis=0)
    grad_bias = lax.dynamic_slice(bias_sum, (place * bias_part,), (bias_part,))
    own_mod = lax.dynamic_index_in_dim(grad_mod, lax.axis_index("rep"), 0, keepdims=False)
    cond_back = contract(own_mod.reshape(fsdp * ITEMS, 6 * D), ada_low, 1, 1)
    cond_back = lax.all_to_all(cond_back.reshape(fsdp, ITEMS, shard), "fsdp", 0, 0, tiled=True)
    grad_cond_act = cond_back.transpose(1, 0, 2).reshape(ITEMS, D)
    sigmoid_c = jax.nn.sigmoid(cond_values)
    grad_condition = (grad_cond_act * sigmoid_c * (1.0 + cond_values * (1.0 - sigmoid_c))).astype(bf16)

    gains = jnp.sum(gain_parts, axis=2)
    gains = butterfly_sum(butterfly_sum(gains, "rep", rep), "fsdp", fsdp)
    return (
        result_tokens,
        stream_grad.astype(bf16)[None],
        grad_condition[None],
        grad_ada,
        grad_bias,
        replica_sum(qkv_sum, rep, 1),
        replica_sum(out_sum, rep, 1),
        replica_sum(gate_up_sum, rep, 1),
        replica_sum(down_sum, rep, 0),
        gains[0],
        gains[1],
    )


def solution(mesh):
    batch = ("fsdp", "rep")
    return jax.shard_map(
        functools.partial(per_device, mesh.shape["fsdp"], mesh.shape["rep"]),
        mesh=mesh,
        in_specs=(
            P(batch, None, None),
            P(batch, None, None),
            P(batch, None),
            P(batch, None),
            P(batch, None),
            P(batch, None),
            P("fsdp", None),
            P("fsdp"),
            P("fsdp", None),
            P("fsdp", None),
            P("fsdp", None),
            P("fsdp", None),
            P(),
            P(),
            P(batch, None, None),
        ),
        out_specs=(
            P(batch, None, None),
            P(batch, None, None),
            P(batch, None, None),
            P("fsdp", None),
            P("fsdp"),
            P("fsdp", None),
            P("fsdp", None),
            P("fsdp", None),
            P("fsdp", None),
            P(),
            P(),
        ),
        check_vma=False,
    )
```

```python
import functools
import math

import jax
import jax.numpy as jnp
from jax import lax
from jax.experimental import pallas as pl
from jax.experimental.pallas import tpu as pltpu
from jax.sharding import PartitionSpec as P
from jax.experimental.layout import Layout, with_layout_constraint

D = 1152
HEADS = 16
HEAD_DIM = 72
SEQ_LEN = 1024
FF = 3072
ITEMS = 4
GRID = 16
epsilon = 1e-06
PAD = 24
FIRST = 256
BLK = 256
SCORE_EXP = HEAD_DIM ** (-0.5) * math.log2(math.e)
f32 = jnp.float32
bf16 = jnp.bfloat16


def dot_nn(a, b):
    return lax.dot_general(a, b, (((1,), (0,)), ((), ())), preferred_element_type=f32)


def dot_nt(a, b):
    return lax.dot_general(a, b, (((1,), (1,)), ((), ())), preferred_element_type=f32)


def block_at(index):
    return pl.ds(pl.multiple_of(index * BLK, BLK), BLK)


def turn(value, roll_ref, cos_t, up_t, down_t, sign):
    roll_ref[PAD : PAD + HEAD_DIM, :] = value
    above = roll_ref[PAD + 18 : PAD + 18 + HEAD_DIM, :]
    below = roll_ref[PAD - 18 : PAD - 18 + HEAD_DIM, :]
    return value * cos_t + sign * (above * up_t + below * down_t)


def normed(raw):
    factor = lax.rsqrt(jnp.sum(raw * raw, axis=0, keepdims=True) * (1.0 / HEAD_DIM) + epsilon)
    return raw * factor, factor


def fill_mask(seg_col_ref, seg_row_ref, mask_ref):
    for start in range(0, SEQ_LEN - FIRST, BLK):
        rows = seg_col_ref[FIRST + start : FIRST + start + BLK, :]
        cols = seg_row_ref[:, FIRST:]
        mask_ref[start : start + BLK, :] = jnp.where(rows == cols, 1.0, 0.0).astype(mask_ref.dtype)


def forward_kernel(q_ref, k_ref, v_ref, gq_ref, gk_ref, cos_ref, up_ref, down_ref, segc_ref, segr_ref,
                   o_ref, inv_ref, mask_ref, roll_ref, qt_ref, kk_ref, vt_ref):
    @pl.when(pl.program_id(0) == 0)
    def _():
        fill_mask(segc_ref, segr_ref, mask_ref)
        roll_ref[...] = jnp.zeros_like(roll_ref)

    for half in range(2):
        def prepare(index, carry):
            at = block_at(index)
            tables = (cos_ref[:, at], up_ref[:, at], down_ref[:, at])
            q_n, _ = normed(q_ref[half, :, at])
            qt_ref[half, :, at] = turn(q_n * gq_ref[...], roll_ref, *tables, 1.0).astype(bf16)
            k_n, _ = normed(k_ref[half, :, at])
            kk = turn(k_n * gk_ref[...], roll_ref, *tables, 1.0)
            kk_ref[half, at, :] = kk.T.astype(bf16)
            vt_ref[half, :, at] = v_ref[half, :, at].astype(bf16)
            return carry

        lax.fori_loop(0, SEQ_LEN // BLK, prepare, 0)

    def attend(at, lo, hi, mask):
        for half in range(2):
            scores = dot_nn(kk_ref[half, lo:hi, :], qt_ref[half, :, at])
            raised = jnp.exp2(scores * SCORE_EXP)
            if mask is not None:
                raised = raised * mask
            inverse = 1.0 / jnp.sum(raised, axis=0, keepdims=True)
            chance = (raised * inverse).astype(bf16)
            result = dot_nn(vt_ref[half, :, lo:hi], chance)
            o_ref[half * HEAD_DIM : (half + 1) * HEAD_DIM, at] = result.astype(bf16)
            inv_ref[half, :, at] = inverse

    attend(pl.ds(0, BLK), 0, FIRST, None)

    def later(index, carry):
        mask = mask_ref[:, block_at(index - 1)].astype(f32)
        attend(block_at(index), FIRST, SEQ_LEN, mask)
        return carry

    lax.fori_loop(1, SEQ_LEN // BLK, later, 0)


def backward_kernel(q_ref, k_ref, v_ref, g_ref, inv_ref, gq_ref, gk_ref, cos_ref, up_ref, down_ref, segc_ref,
                    segr_ref, d_ref, gain_ref, mask_ref, roll_ref, qt_ref, kt_ref, kk_ref, vv_ref,
                    dq_ref, dk_ref, dv_ref):
    @pl.when(pl.program_id(0) == 0)
    def _():
        fill_mask(segc_ref, segr_ref, mask_ref)
        roll_ref[...] = jnp.zeros_like(roll_ref)
        gain_ref[...] = jnp.zeros_like(gain_ref)

    for half in range(2):
        def prepare(index, carry):
            at = block_at(index)
            tables = (cos_ref[:, at], up_ref[:, at], down_ref[:, at])
            q_n, _ = normed(q_ref[half, :, at])
            qt_ref[half, :, at] = turn(q_n * gq_ref[...], roll_ref, *tables, 1.0).astype(bf16)
            k_n, _ = normed(k_ref[half, :, at])
            kk = turn(k_n * gk_ref[...], roll_ref, *tables, 1.0)
            kt_ref[half, :, at] = kk.astype(bf16)
            kk_ref[half, at, :] = kk.T.astype(bf16)
            vv_ref[half, at, :] = v_ref[half, :, at].T.astype(bf16)
            return carry

        lax.fori_loop(0, SEQ_LEN // BLK, prepare, 0)

    def attend(at, lo, hi, mask, first):
        for half in range(2):
            rows = slice(half * HEAD_DIM, (half + 1) * HEAD_DIM)
            q_b = qt_ref[half, :, at]
            g_b = g_ref[rows, at]
            scores = dot_nn(kk_ref[half, lo:hi, :], q_b)
            chance = jnp.exp2(scores * SCORE_EXP) * inv_ref[half, :, at]
            if mask is not None:
                chance = chance * mask
            grad_chance = dot_nn(vv_ref[half, lo:hi, :], g_b)
            delta = jnp.sum(chance * grad_chance, axis=0, keepdims=True)
            grad_scores = (chance * (grad_chance - delta)).astype(bf16)
            grad_v = dot_nt(g_b, chance.astype(bf16))
            grad_k = dot_nt(q_b, grad_scores)
            dq_ref[half, :, at] = dot_nn(kt_ref[half, :, lo:hi], grad_scores)
            if first:
                dv_ref[half, :, lo:hi] = grad_v
                dk_ref[half, :, lo:hi] = grad_k
            else:
                dv_ref[half, :, lo:hi] += grad_v
                dk_ref[half, :, lo:hi] += grad_k

    attend(pl.ds(0, BLK), 0, FIRST, None, True)
    dk_ref[:, :, FIRST:] = jnp.zeros((2, HEAD_DIM, SEQ_LEN - FIRST), f32)
    dv_ref[:, :, FIRST:] = jnp.zeros((2, HEAD_DIM, SEQ_LEN - FIRST), f32)

    def later(index, carry):
        mask = mask_ref[:, block_at(index - 1)].astype(f32)
        attend(block_at(index), FIRST, SEQ_LEN, mask, False)
        return carry

    lax.fori_loop(1, SEQ_LEN // BLK, later, 0)

    for half in range(2):
        rows = slice(half * HEAD_DIM, (half + 1) * HEAD_DIM)

        def finish(index, carry):
            at = block_at(index)
            tables = (cos_ref[:, at], up_ref[:, at], down_ref[:, at])
            for which, (raw_ref, grad_ref, weight_ref) in enumerate(((q_ref, dq_ref, gq_ref), (k_ref, dk_ref, gk_ref))):
                unit, factor = normed(raw_ref[half, :, at])
                grad = turn(grad_ref[half, :, at] * (HEAD_DIM ** -0.5), roll_ref, *tables, -1.0)
                part = grad * unit
                gain_ref[which] += part[:, :128] + part[:, 128:]
                grad = grad * weight_ref[...]
                mean = jnp.sum(grad * unit, axis=0, keepdims=True) * (1.0 / HEAD_DIM)
                d_ref[which, rows, at] = (factor * (grad - unit * mean)).astype(bf16)
            d_ref[2, rows, at] = dv_ref[half, :, at].astype(bf16)
            return carry

        lax.fori_loop(0, SEQ_LEN // BLK, finish, 0)


def whole(shape):
    return pl.BlockSpec(shape, lambda h: (0,) * len(shape))


def head_specs():
    return [pl.BlockSpec((2, HEAD_DIM, SEQ_LEN), lambda h, base=base: (base + h, 0, 0)) for base in (0, 8, 16)]


def table_specs():
    return [
        whole((HEAD_DIM, 1)), whole((HEAD_DIM, 1)),
        whole((HEAD_DIM, SEQ_LEN)), whole((HEAD_DIM, SEQ_LEN)), whole((HEAD_DIM, SEQ_LEN)),
        whole((SEQ_LEN, 1)), whole((1, SEQ_LEN)),
    ]


def work_scratch():
    return [
        pltpu.VMEM((SEQ_LEN - FIRST, SEQ_LEN - FIRST), bf16),
        pltpu.VMEM((HEAD_DIM + 2 * PAD, BLK), f32),
    ]


PAIR = (2, HEAD_DIM, SEQ_LEN)
TOKEN_PAIR = (2, SEQ_LEN, HEAD_DIM)


def attention_forward(raw, tables):
    return pl.pallas_call(
        forward_kernel,
        grid=(HEADS // 2,),
        in_specs=head_specs() + table_specs(),
        out_specs=[
            pl.BlockSpec((2 * HEAD_DIM, SEQ_LEN), lambda h: (h, 0)),
            pl.BlockSpec((2, 1, SEQ_LEN), lambda h: (h, 0, 0)),
        ],
        out_shape=[
            jax.ShapeDtypeStruct((D, SEQ_LEN), bf16),
            jax.ShapeDtypeStruct((HEADS, 1, SEQ_LEN), f32),
        ],
        scratch_shapes=work_scratch() + [
            pltpu.VMEM(PAIR, bf16), pltpu.VMEM(TOKEN_PAIR, bf16), pltpu.VMEM(PAIR, bf16),
        ],
        cost_estimate=pl.CostEstimate(flops=14_000_000_000, bytes_accessed=20_000_000, transcendentals=10_500_000),
        name="attend",
    )(raw, raw, raw, *tables)


def attention_backward(raw, grad_t, inverse, tables):
    return pl.pallas_call(
        backward_kernel,
        grid=(HEADS // 2,),
        in_specs=head_specs() + [
            pl.BlockSpec((2 * HEAD_DIM, SEQ_LEN), lambda h: (h, 0)),
            pl.BlockSpec((2, 1, SEQ_LEN), lambda h: (h, 0, 0)),
        ] + table_specs(),
        out_specs=[
            pl.BlockSpec((3, 2 * HEAD_DIM, SEQ_LEN), lambda h: (0, h, 0)),
            whole((2, HEAD_DIM, 128)),
        ],
        out_shape=[
            jax.ShapeDtypeStruct((3, D, SEQ_LEN), bf16),
            jax.ShapeDtypeStruct((2, HEAD_DIM, 128), f32),
        ],
        scratch_shapes=work_scratch() + [
            pltpu.VMEM(PAIR, bf16), pltpu.VMEM(PAIR, bf16), pltpu.VMEM(TOKEN_PAIR, bf16), pltpu.VMEM(TOKEN_PAIR, bf16),
            pltpu.VMEM(PAIR, f32), pltpu.VMEM(PAIR, f32), pltpu.VMEM(PAIR, f32),
        ],
        cost_estimate=pl.CostEstimate(flops=35_000_000_000, bytes_accessed=25_000_000, transcendentals=10_500_000),
        name="attend_back",
    )(raw, raw, raw, grad_t, inverse, *tables)


def product(left, right):
    return jnp.dot(left, right, preferred_element_type=f32)


def contract(left, right, left_dim, right_dim):
    return lax.dot_general(left, right, (((left_dim,), (right_dim,)), ((), ())), preferred_element_type=f32)


def angle_tables(heights, widths, lengths, segments):
    ends = jnp.cumsum(lengths)
    starts = ends - lengths
    places = jnp.arange(SEQ_LEN, dtype=jnp.int32)
    member = segments[:, None] == jnp.arange(ITEMS, dtype=jnp.int32)[None, :]
    start_tok = jnp.sum(jnp.where(member, starts[None, :], 0), axis=1)
    width_tok = jnp.sum(jnp.where(member, widths[None, :], 0), axis=1)
    height_tok = jnp.sum(jnp.where(member, heights[None, :], 0), axis=1)
    inside = width_tok > 0
    offset = places - start_tok
    safe_width = jnp.maximum(width_tok, 1)
    safe_height = jnp.maximum(height_tok, 1)
    row_index = jnp.where(inside, offset // safe_width, 0)
    col_index = jnp.where(inside, offset % safe_width, 0)
    height_f = safe_height.astype(f32)
    width_f = safe_width.astype(f32)
    row_place = jnp.where(inside, (row_index.astype(f32) - 0.5 * (height_f - 1.0)) * (GRID / height_f), 0.0)
    col_place = jnp.where(inside, (col_index.astype(f32) - 0.5 * (width_f - 1.0)) * (GRID / width_f), 0.0)
    quarter = HEAD_DIM // 4
    lane = jnp.arange(HEAD_DIM, dtype=jnp.int32)
    freqs = jnp.exp((lane % quarter).astype(f32) * (-math.log(10000.0) / quarter))
    place = jnp.where((lane < 2 * quarter)[:, None], row_place[None, :], col_place[None, :])
    angle = place * freqs[:, None]
    cos_t = jnp.cos(angle)
    sin_t = jnp.sin(angle)
    leading = (lane // quarter % 2 == 0)[:, None]
    return cos_t, jnp.where(leading, -sin_t, 0.0), jnp.where(leading, 0.0, sin_t)


def rms_scale(values):
    return lax.rsqrt(jnp.mean(values * values, axis=-1, keepdims=True) + epsilon)


def rms_back(grad_normed, normed_values, factor):
    return factor * (grad_normed - normed_values * jnp.mean(grad_normed * normed_values, axis=-1, keepdims=True))


barrier = lax.optimization_barrier


def flip(array, axis, size, bit):
    return lax.ppermute(array, axis, [(i, i ^ bit) for i in range(size)])


def bits_of(size):
    return [1 << b for b in range(size.bit_length() - 1)]


def gather_steps(array, axis, size, dim):
    for bit in bits_of(size):
        array = jnp.concatenate([array, flip(array, axis, size, bit)], axis=dim)
    return array


def scatter_steps(array, axis, size):
    place = lax.axis_index(axis)
    for bit in bits_of(size):
        low = (place & bit) == 0
        pairs = array.reshape((array.shape[0] // 2, 2) + array.shape[1:])
        even, odd = pairs[:, 0], pairs[:, 1]
        received = flip(jnp.where(low, odd, even), axis, size, bit)
        array = jnp.where(low, even, odd) + received
    return array[0]


def line_steps(size):
    inner = size // 2 - 1

    def inward(step, array):
        return array + lax.ppermute(array, "rep", [(step, step + 1), (size - 1 - step, size - 2 - step)])

    def middle(array):
        return array + lax.ppermute(array, "rep", [(inner, inner + 1), (inner + 1, inner)])

    def outward(step, array):
        place = lax.axis_index("rep")
        received = lax.ppermute(array, "rep", [(step + 1, step), (size - 2 - step, size - 1 - step)])
        return jnp.where((place == step) | (place == size - 1 - step), received, array)

    return (
        [functools.partial(inward, step) for step in range(inner)]
        + [middle]
        + [functools.partial(outward, step) for step in reversed(range(inner))]
    )


class Line:
    def __init__(self, array, size):
        self.array = array
        self.steps = line_steps(size)

    def advance(self):
        if self.steps:
            self.array = self.steps.pop(0)(self.array)

    def total(self):
        while self.steps:
            self.advance()
        return self.array.astype(f32)


def meet(value, lines):
    value, arrays = barrier((value, [line.array for line in lines]))
    for line, array in zip(lines, arrays):
        line.array = array
        line.advance()
    return value


def thirds(values):
    parts = []
    for _ in range(3):
        part = lax.reduce_precision(values, 8, 7)
        parts.append(part.astype(bf16))
        values = values - part
    return jnp.stack(parts)


def per_device(
    fsdp,
    rep,
    tokens,
    condition,
    heights,
    widths,
    lengths,
    segments,
    ada_weight,
    ada_bias,
    qkv_weight,
    out_weight,
    gate_up_weight,
    down_weight,
    query_gain,
    key_gain,
    cotangent,
):
    place = lax.axis_index("fsdp")
    segment = segments[0]

    def gathered(weight):
        return lax.all_gather(weight.astype(bf16), "fsdp", axis=0, tiled=True)

    def scattered(grad):
        return lax.psum_scatter(grad.astype(bf16), "fsdp", scatter_dimension=0, tiled=True)

    qkv_full = gathered(qkv_weight)
    out_full = gathered(out_weight)
    gate_up_full = gathered(gate_up_weight)
    down_full = gathered(down_weight)

    shard = ada_weight.shape[0]
    cond_values = condition[0].astype(f32)
    cond_act = jax.nn.silu(cond_values).astype(bf16)
    cond_parts = cond_act.reshape(ITEMS, fsdp, shard).transpose(1, 0, 2)
    cond_cols = lax.all_to_all(cond_parts, "fsdp", 0, 0, tiled=True)
    ada_low = ada_weight.astype(bf16)
    partial = product(cond_cols.reshape(fsdp * ITEMS, shard), ada_low)
    bias_part = ada_bias.shape[0]
    bias_row = lax.dynamic_update_slice(
        jnp.zeros((6 * D,), f32), ada_bias.astype(bf16).astype(f32), (place * bias_part,)
    )
    modulation = scatter_steps((partial + bias_row[None, :]).reshape(fsdp, ITEMS, 6 * D), "fsdp", fsdp)

    segment_col = segment[:, None]

    def spread(which):
        rows = modulation[:, which * D : (which + 1) * D]
        result = jnp.zeros((SEQ_LEN, D), f32)
        for item in range(ITEMS):
            result = jnp.where(segment_col == item, rows[item][None, :], result)
        return result

    shift_a, scale_a, gate_a, shift_b, scale_b, gate_b = [spread(which) for which in range(6)]
    stream = tokens[0].astype(f32)
    factor_a = rms_scale(stream)
    normed_a = stream * factor_a
    hidden_a = barrier((normed_a * (1.0 + scale_a) + shift_a).astype(bf16))
    raw = with_layout_constraint(contract(qkv_full, hidden_a, 0, 1), Layout((0, 1)))
    raw = raw.reshape(3 * HEADS, HEAD_DIM, SEQ_LEN)
    tables = (
        query_gain[:, None],
        key_gain[:, None],
        *angle_tables(heights[0], widths[0], lengths[0], segment),
        segment_col,
        segment[None, :],
    )
    attended_t, inverse = attention_forward(raw, tables)
    branch_a = contract(attended_t, out_full, 0, 0)
    stream_b = stream + gate_a * branch_a
    factor_b = rms_scale(stream_b)
    normed_b = stream_b * factor_b
    hidden_b = barrier((normed_b * (1.0 + scale_b) + shift_b).astype(bf16))
    gate_up = product(hidden_b, gate_up_full)
    gate_val = gate_up[:, :FF]
    up_val = gate_up[:, FF:]
    sigmoid_g = jax.nn.sigmoid(gate_val)
    inner = (gate_val * sigmoid_g * up_val).astype(bf16)
    branch_b = product(inner, down_full)
    result_tokens = (stream_b + gate_b * branch_b).astype(bf16)[None]

    upstream = cotangent[0].astype(f32)
    grad_gate_b = upstream * branch_b
    grad_branch_b = barrier((upstream * gate_b).astype(bf16))
    grad_inner = contract(grad_branch_b, down_full, 1, 1)
    grad_down = contract(inner, grad_branch_b, 0, 0).astype(bf16)
    grad_gate_act = (grad_inner * up_val * sigmoid_g * (1.0 + gate_val * (1.0 - sigmoid_g))).astype(bf16)
    grad_up_act = (grad_inner * gate_val * sigmoid_g).astype(bf16)
    grad_gate_act, grad_up_act, grad_down = barrier((grad_gate_act, grad_up_act, grad_down))
    down_line = Line(scattered(grad_down), rep)
    grad_gate = contract(hidden_b, grad_gate_act, 0, 0).astype(bf16)
    grad_up = contract(hidden_b, grad_up_act, 0, 0).astype(bf16)
    grad_gate_act, grad_up_act, grad_gate, grad_up = barrier((grad_gate_act, grad_up_act, grad_gate, grad_up))
    gate_line = Line(scattered(grad_gate), rep)
    up_line = Line(scattered(grad_up), rep)
    grad_hidden_b = contract(jnp.concatenate([grad_gate_act, grad_up_act], axis=1), gate_up_full, 1, 1)
    grad_scale_b = grad_hidden_b * normed_b
    grad_stream_b = upstream + rms_back(grad_hidden_b * (1.0 + scale_b), normed_b, factor_b)
    grad_gate_a = grad_stream_b * branch_a
    grad_branch_a = (grad_stream_b * gate_a).astype(bf16)
    grad_branch_a = meet(grad_branch_a, [down_line])
    grad_out = product(attended_t, grad_branch_a).astype(bf16)
    grad_attended_t = contract(out_full, grad_branch_a, 1, 1).astype(bf16)
    grad_attended_t, grad_out = barrier((grad_attended_t, grad_out))
    out_line = Line(scattered(grad_out), rep)
    grad_raw, gain_parts = attention_backward(raw, grad_attended_t, inverse, tables)
    grad_raw = meet(grad_raw, [down_line, gate_line]).reshape(3 * D, SEQ_LEN)
    grad_qkv = [contract(hidden_a, grad_raw[which * D : (which + 1) * D], 0, 1).astype(bf16) for which in range(3)]
    grad_raw, grad_qkv = barrier((grad_raw, grad_qkv))
    qkv_lines = [Line(scattered(part), rep) for part in grad_qkv]
    grad_hidden_a = contract(grad_raw, qkv_full, 0, 1)
    grad_hidden_a = meet(grad_hidden_a, [down_line, gate_line, up_line])
    stream_grad = grad_stream_b + rms_back(grad_hidden_a * (1.0 + scale_a), normed_a, factor_a)

    member = (segment[None, :] == jnp.arange(ITEMS, dtype=jnp.int32)[:, None]).astype(f32)

    def collect(piece):
        return jnp.dot(member, piece, precision=lax.Precision.HIGHEST).astype(bf16)

    def all_devices(block):
        return gather_steps(gather_steps(block[None, None], "rep", rep, 0), "fsdp", fsdp, 1)

    late_mod = all_devices(
        jnp.concatenate([collect(p) for p in (grad_gate_a, grad_hidden_b, grad_scale_b, grad_gate_b)], axis=1)
    )
    gains = thirds(jnp.sum(gain_parts, axis=2)).reshape(ITEMS, -1)
    width = gains.shape[1]
    early_mod = all_devices(
        jnp.concatenate(
            [collect(grad_hidden_a), collect(grad_hidden_a * normed_a), jnp.pad(gains, ((0, 0), (0, 128 - width)))],
            axis=1,
        )
    )
    images = rep * fsdp * ITEMS
    flat_mod = jnp.concatenate([early_mod[..., : 2 * D], late_mod], axis=3).reshape(images, 6 * D)
    cond_rel = jnp.take(cond_cols, place ^ jnp.arange(fsdp), axis=0)
    cond_all = gather_steps(cond_rel[None], "rep", rep, 0)
    grad_ada = contract(cond_all.reshape(images, shard), flat_mod, 0, 0)
    bias_sum = jnp.sum(flat_mod.astype(f32), axis=0)
    grad_bias = lax.dynamic_slice(bias_sum, (place * bias_part,), (bias_part,))
    cond_back = contract(flat_mod[: fsdp * ITEMS], ada_low, 1, 1).reshape(fsdp, ITEMS, shard)
    cond_back = lax.all_to_all(jnp.take(cond_back, place ^ jnp.arange(fsdp), axis=0), "fsdp", 0, 0, tiled=True)
    grad_cond_act = cond_back.transpose(1, 0, 2).reshape(ITEMS, D)
    sigmoid_c = jax.nn.sigmoid(cond_values)
    grad_condition = (grad_cond_act * sigmoid_c * (1.0 + cond_values * (1.0 - sigmoid_c))).astype(bf16)

    every = early_mod[..., 2 * D : 2 * D + width].reshape(rep, fsdp, 3, -1).astype(f32)
    every = jnp.take(every, lax.axis_index("rep") ^ jnp.arange(rep), axis=0)
    every = jnp.take(every, place ^ jnp.arange(fsdp), axis=1)
    gain_sums = jnp.sum(every, axis=(0, 1, 2)).reshape(2, HEAD_DIM)
    return (
        result_tokens,
        stream_grad.astype(bf16)[None],
        grad_condition[None],
        grad_ada,
        grad_bias,
        jnp.concatenate([line.total() for line in qkv_lines], axis=1),
        out_line.total(),
        jnp.concatenate([gate_line.total(), up_line.total()], axis=1),
        down_line.total(),
        gain_sums[0],
        gain_sums[1],
    )


def solution(mesh):
    batch = ("fsdp", "rep")
    return jax.shard_map(
        functools.partial(per_device, mesh.shape["fsdp"], mesh.shape["rep"]),
        mesh=mesh,
        in_specs=(
            P(batch, None, None),
            P(batch, None, None),
            P(batch, None),
            P(batch, None),
            P(batch, None),
            P(batch, None),
            P("fsdp", None),
            P("fsdp"),
            P("fsdp", None),
            P("fsdp", None),
            P("fsdp", None),
            P("fsdp", None),
            P(),
            P(),
            P(batch, None, None),
        ),
        out_specs=(
            P(batch, None, None),
            P(batch, None, None),
            P(batch, None, None),
            P("fsdp", None),
            P("fsdp"),
            P("fsdp", None),
            P("fsdp", None),
            P("fsdp", None),
            P("fsdp", None),
            P(),
            P(),
        ),
        check_vma=False,
    )
```
